32 devices in a mesh: groups: 2 (over y), row: 16 (over z, x, core).
Axes of the slice: x: 2, y: 2, z: 4, core: 2. Of those that a mesh axis runs over, the one named last changes fastest.
Arguments:
- left_features: bfloat16 [96, 4096], P(('groups', 'row')), parts along dimension 0, may hold values from -24 to 24
- right_features: bfloat16 [96, 4096], P(('groups', 'row')), parts along dimension 0, may hold values from -24 to 24
- alignment_mask: int32 [96, 128], P(('groups', 'row')), parts along dimension 0, may hold values from 0 to 1, as said below
- projection_weight: bfloat16 [1024, 128], replicated, may hold values from -0.1875 to 0.1875
- projection_bias: float32 [128], replicated, may hold values from -6 to 6
- pair_output_cotangent: bfloat16 [96, 48, 128], P(('groups', 'row')), parts along dimension 0, may hold values from -6 to 6
Outputs:
- pair_out: bfloat16 [96, 48, 128], P(('groups', 'row')), parts along dimension 0
- left_feature_gradient: float32 [96, 4096], P(('groups', 'row')), parts along dimension 0
- right_feature_gradient: float32 [96, 4096], P(('groups', 'row')), parts along dimension 0
- grad_weight: float32 [2048, 128], P('groups'), parts along dimension 0
- grad_bias: float32 [256], P('groups'), parts along dimension 0
The draws below stay inside these ranges and needn't reach their ends.
There are 2 independent parts, one for each index of `groups`. The reference program is written for one: setup_inputs(seed, part) draws one part's arguments, and reference() takes and returns one part's arrays. A program takes and returns all parts, laid end to end along the dimension named above; an argument that names none is the same for every part. Nothing has to cross between parts.
Inputs may be any that keep to these rules, and one draw needn't show every extreme that they name: `alignment_mask`: each protein is present up to some length and padded after it: from some residue on to the last, all entries are 0; that length lies between 36 and 47.
All inputs are finite; a program needn't handle non-finite values.
Results may differ from the reference program's by a relative error of at most 0.0041.
Values may be sent and summed in bfloat16 or wider, within the bound.
No kernel may reach another device: no remote copies, remote signals or barrier semaphores. Data moves between devices by JAX's collectives and lax.ppermute only.
A program may use at most 128 MiB of HBM per device.

```python
import math
import jax
import jax.numpy as jnp
from jax import lax

ALIGNMENT_ROWS = 128
FEATURE_CHANNELS = 32
PAIR_CHANNELS = 128
RESIDUE_COUNT = 48


def draw_alignment_mask(key, part):
    key_len, random_key_bits = jax.random.split(jax.random.fold_in(key, 17))
    valid_len = jax.random.randint(key_len, (), RESIDUE_COUNT - RESIDUE_COUNT // 4, RESIDUE_COUNT)
    retained_random_bits = jax.random.randint(random_key_bits, (RESIDUE_COUNT, ALIGNMENT_ROWS), 0, 20) < 17
    block_position = lax.broadcasted_iota(jnp.int32, (RESIDUE_COUNT, ALIGNMENT_ROWS), 0)
    return (retained_random_bits & (block_position < valid_len)).astype(jnp.int32)


def strengthened(drawn, key, source, target, parts, factor):
    def block_of(dim):
        return (jnp.arange(drawn.shape[dim]) // (drawn.shape[dim] // parts)).reshape((-1,) + (1,) * (drawn.ndim - 1 - dim))

    near = jax.random.permutation(key, parts)[block_of(target)]
    second = (block_of(target) + parts // 2) % parts
    return jnp.where((block_of(source) == near) | (block_of(source) == second), factor * drawn, drawn)


def block_scale(rng, dims, shards, smallest, largest):
    def one(dim, shards_of):
        draws = jax.random.uniform(jax.random.fold_in(jax.random.fold_in(rng, 6), dim), (shards_of,), jnp.float32, smallest / len(shards), largest / len(shards))
        return jnp.repeat(jnp.exp(draws), dims[dim] // shards_of).reshape((-1,) + (1,) * (len(dims) - dim - 1))

    factor_of = one(*shards[0])
    for cut in shards[1:]:
        factor_of = factor_of * one(*cut)
    return factor_of


def gaussian(own_key, dims, scale, bound, shards=(), kind=jnp.bfloat16):
    result = scale * jax.random.normal(own_key, dims, jnp.float32)
    if shards:
        result = result * block_scale(own_key, dims, shards, -0.22, 0.18)
    return jnp.clip(result, -bound, bound).astype(kind)


def noise_with(stream_key, extent, spread, most, pieces, heavy, held_as=jnp.bfloat16):
    array = spread * jax.random.normal(stream_key, extent, jnp.float32)
    if pieces:
        array = array * block_scale(stream_key, extent, pieces, -0.22, 0.18)
    return jnp.clip(strengthened(array, jax.random.fold_in(stream_key, 3), *heavy), -most, most).astype(held_as)


def setup_inputs(seed: int = 0, part: int = 0) -> dict:
    key_of = jax.random.split(jax.random.key(seed), 7)
    part_keys = jax.random.split(jax.random.fold_in(key_of[6], part), 7)
    return {
        "left_features": gaussian(part_keys[0], (RESIDUE_COUNT, ALIGNMENT_ROWS * FEATURE_CHANNELS), 4.0, 24.0, ((0, 16),)),
        "right_features": gaussian(part_keys[1], (RESIDUE_COUNT, ALIGNMENT_ROWS * FEATURE_CHANNELS), 4.0, 24.0, ((0, 16),)),
        "alignment_mask": draw_alignment_mask(jax.random.fold_in(jax.random.fold_in(key_of[6], part), 71), part),
        "projection_weight": gaussian(key_of[3], (FEATURE_CHANNELS * FEATURE_CHANNELS, PAIR_CHANNELS), (FEATURE_CHANNELS * FEATURE_CHANNELS) ** -0.5, 0.1875),
        "projection_bias": gaussian(key_of[4], (PAIR_CHANNELS,), 1.0, 6.0, (), jnp.float32),
        "pair_output_cotangent": noise_with(part_keys[5], (RESIDUE_COUNT, RESIDUE_COUNT, PAIR_CHANNELS), 1.0, 6.0, ((0, 16),), (0, 1, 16, 2.0)),
    }


def reference(left_features, right_features, alignment_mask, projection_weight, projection_bias, pair_output_cotangent):
    hp = lax.Precision.HIGHEST
    mask_float = alignment_mask.astype(jnp.float32)
    left_masked = left_features.astype(jnp.float32).reshape(RESIDUE_COUNT, ALIGNMENT_ROWS, FEATURE_CHANNELS) * mask_float[:, :, None]
    right_masked = right_features.astype(jnp.float32).reshape(RESIDUE_COUNT, ALIGNMENT_ROWS, FEATURE_CHANNELS) * mask_float[:, :, None]
    counts = jnp.dot(mask_float, mask_float.T, precision=hp)
    pair_norm = jnp.maximum(counts, 1.0)
    rows_per_block = math.gcd(RESIDUE_COUNT, 32)
    number_of_blocks = RESIDUE_COUNT // rows_per_block
    weight_f = projection_weight

    def block_step(state_carry, index):
        right_accumulator, weight_acc, bias_acc = state_carry
        first = index * rows_per_block
        left_blk = lax.dynamic_slice_in_dim(left_masked, first, rows_per_block, 0)
        norm_blk = lax.dynamic_slice_in_dim(pair_norm, first, rows_per_block, 0)[:, :, None]
        cot_blk = lax.dynamic_slice_in_dim(pair_output_cotangent, first, rows_per_block, 0)
        outer_prod = jnp.einsum('isc,jse->ijce', left_blk, right_masked, precision=hp).reshape(rows_per_block, RESIDUE_COUNT, FEATURE_CHANNELS * FEATURE_CHANNELS)
        prob = (outer_prod / norm_blk).astype(jnp.bfloat16)
        flat_prob = prob.reshape(rows_per_block * RESIDUE_COUNT, FEATURE_CHANNELS * FEATURE_CHANNELS)
        cot_flat = cot_blk.reshape(rows_per_block * RESIDUE_COUNT, PAIR_CHANNELS)
        pair_block = (jnp.dot(flat_prob, weight_f, preferred_element_type=jnp.float32) + projection_bias).astype(jnp.bfloat16)
        prob_grad = jnp.dot(cot_flat, weight_f.T, preferred_element_type=jnp.float32).reshape(rows_per_block, RESIDUE_COUNT, FEATURE_CHANNELS * FEATURE_CHANNELS)
        outer_grad = (prob_grad / norm_blk).astype(jnp.bfloat16).astype(jnp.float32).reshape(rows_per_block, RESIDUE_COUNT, FEATURE_CHANNELS, FEATURE_CHANNELS)
        left_grad = jnp.einsum('ijce,jse->isc', outer_grad, right_masked, precision=hp)
        right_accumulator = right_accumulator + jnp.einsum('ijce,isc->jse', outer_grad, left_blk, precision=hp)
        weight_acc = weight_acc + jnp.dot(flat_prob.T, cot_flat, preferred_element_type=jnp.float32)
        bias_acc = bias_acc + jnp.sum(cot_flat.astype(jnp.float32), axis=0)
        return (right_accumulator, weight_acc, bias_acc), (pair_block.reshape(rows_per_block, RESIDUE_COUNT, PAIR_CHANNELS), left_grad)

    starting_carry = (jnp.zeros((RESIDUE_COUNT, ALIGNMENT_ROWS, FEATURE_CHANNELS), jnp.float32), jnp.zeros((FEATURE_CHANNELS * FEATURE_CHANNELS, PAIR_CHANNELS), jnp.float32), jnp.zeros((PAIR_CHANNELS,), jnp.float32))
    (right_accumulator, weight_acc, bias_acc), (pairs, left_gradient_parts) = lax.scan(block_step, starting_carry, jnp.arange(number_of_blocks, dtype=jnp.int32))
    pair_out = pairs.reshape(RESIDUE_COUNT, RESIDUE_COUNT, PAIR_CHANNELS)
    left_feature_gradient = (left_gradient_parts.reshape(RESIDUE_COUNT, ALIGNMENT_ROWS, FEATURE_CHANNELS) * mask_float[:, :, None]).reshape(RESIDUE_COUNT, ALIGNMENT_ROWS * FEATURE_CHANNELS)
    right_feature_gradient = (right_accumulator * mask_float[:, :, None]).reshape(RESIDUE_COUNT, ALIGNMENT_ROWS * FEATURE_CHANNELS)
    return pair_out, left_feature_gradient, right_feature_gradient, weight_acc / RESIDUE_COUNT, bias_acc / RESIDUE_COUNT
```

```python
import math

import jax
import jax.numpy as jnp
from jax import lax
from jax.experimental import pallas as pl
from jax.experimental.pallas import tpu as pltpu
from jax.sharding import PartitionSpec as P

LANES = 128
SUBLANES = 16


def reduced(
    left_features,
    right_features,
    alignment_mask,
    projection_weight,
    projection_bias,
    pair_output_cotangent,
):
    shard_rows, row_channel_width = left_features.shape
    alignment_depth = alignment_mask.shape[1]
    channel_count = row_channel_width // alignment_depth
    hidden_width = projection_weight.shape[0]
    pair_width = projection_weight.shape[1]
    mask_halfwidth = alignment_mask.astype(jnp.bfloat16)
    shard_mask = alignment_mask.astype(jnp.float32)
    left_masked = (
        left_features.reshape(shard_rows, alignment_depth, channel_count)
        * mask_halfwidth[:, :, None]
    )
    right_masked = (
        right_features.reshape(shard_rows, alignment_depth, channel_count)
        * mask_halfwidth[:, :, None]
    ).reshape(shard_rows, row_channel_width)
    gathered_right, gathered_mask = (
        lax.all_gather(right_masked, "row", axis=0, tiled=True),
        lax.all_gather(mask_halfwidth, "row", axis=0, tiled=True),
    )
    residues = gathered_right.shape[0]
    rows_per_block = math.gcd(residues, 128)
    number_of_blocks = residues // rows_per_block
    right_block_list = gathered_right.reshape(
        number_of_blocks, rows_per_block, alignment_depth, channel_count
    )
    mask_block_list = gathered_mask.reshape(number_of_blocks, rows_per_block, alignment_depth)
    cot_blocks = pair_output_cotangent.reshape(
        shard_rows, number_of_blocks, rows_per_block, pair_width
    ).transpose(1, 0, 2, 3)

    def block_step(state_carry, inputs):
        left_acc, weight_acc, bias_acc = state_carry
        right_blk, mask_blk, cot_blk = inputs
        counts = jnp.dot(
            shard_mask, mask_blk.astype(jnp.float32).T, precision=lax.Precision.HIGHEST
        )
        pair_norm = jnp.maximum(counts, 1.0)[:, :, None]
        outer_prod = jnp.einsum(
            "isc,jse->ijce", left_masked, right_blk, preferred_element_type=jnp.float32
        ).reshape(shard_rows, rows_per_block, hidden_width)
        prob = (outer_prod / pair_norm).astype(jnp.bfloat16)
        flat_prob = prob.reshape(shard_rows * rows_per_block, hidden_width)
        cot_flat = cot_blk.reshape(shard_rows * rows_per_block, pair_width)
        pair_block = (
            jnp.dot(flat_prob, projection_weight, preferred_element_type=jnp.float32)
            + projection_bias
        ).astype(jnp.bfloat16)
        prob_grad = lax.dot_general(
            cot_flat,
            projection_weight,
            (((1,), (1,)), ((), ())),
            preferred_element_type=jnp.float32,
        )
        outer_grad = (
            prob_grad.reshape(shard_rows, rows_per_block, hidden_width) / pair_norm
        ).astype(jnp.bfloat16)
        left_acc = left_acc + jnp.einsum(
            "ijce,jse->isc",
            outer_grad.reshape(shard_rows, rows_per_block, channel_count, channel_count),
            right_blk,
            preferred_element_type=jnp.float32,
        )
        weight_acc = weight_acc + lax.dot_general(
            flat_prob, cot_flat, (((0,), (0,)), ((), ())), preferred_element_type=jnp.float32
        )
        bias_acc = bias_acc + jnp.sum(cot_flat.astype(jnp.float32), axis=0)
        return (
            (left_acc, weight_acc, bias_acc),
            (pair_block.reshape(shard_rows, rows_per_block, pair_width), outer_grad),
        )

    starting_carry = (
        jnp.zeros((shard_rows, alignment_depth, channel_count), jnp.float32),
        jnp.zeros((hidden_width, pair_width), jnp.float32),
        jnp.zeros((pair_width,), jnp.float32),
    )
    (left_acc, weight_acc, bias_acc), (pairs, grads_out) = lax.scan(
        block_step, starting_carry, (right_block_list, mask_block_list, cot_blocks)
    )
    pair_out = pairs.transpose(1, 0, 2, 3).reshape(shard_rows, residues, pair_width)
    outer_all = grads_out.transpose(1, 0, 2, 3).reshape(
        shard_rows, residues, channel_count, channel_count
    )
    weight_sum, bias_sum = lax.psum((weight_acc, bias_acc), "row")
    left_feature_gradient = (left_acc * shard_mask[:, :, None]).reshape(
        shard_rows, row_channel_width
    )
    result = jnp.einsum("ijce,isc->jse", outer_all, left_masked, preferred_element_type=jnp.float32)
    right_accumulator = lax.psum_scatter(
        result.reshape(shard_rows * lax.axis_size("row"), row_channel_width),
        "row",
        scatter_dimension=0,
        tiled=True,
    ).reshape(shard_rows, alignment_depth, channel_count)
    right_feature_gradient = (right_accumulator * shard_mask[:, :, None]).reshape(
        shard_rows, row_channel_width
    )
    return (
        pair_out,
        left_feature_gradient,
        right_feature_gradient,
        weight_sum / residues,
        bias_sum / residues,
    )


def rounded_up(count, step):
    return -(-count // step) * step


def fits(devices, left, right, mask, weight, bias, cotangent):
    rows, depth = mask.shape
    channels = left.shape[1] // depth
    return (
        depth == LANES
        and weight.shape[1] == LANES
        and weight.shape[0] == channels * channels
        and LANES % channels == 0
        and channels % SUBLANES == 0
        and rows * devices == cotangent.shape[1]
        and 2 * cotangent.shape[1] <= LANES
        and cotangent.shape[1] % SUBLANES == 0
        and devices & (devices - 1) == 0
    )


def dot(a, b, dims):
    return lax.dot_general(a, b, (dims, ((), ())), preferred_element_type=jnp.float32)


def message_layout(rows, channels, residues):
    right = rows * channels
    cotangent = 2 * rows * channels
    mask = cotangent + rows * residues
    return right, cotangent, mask, mask + rounded_up(rows, SUBLANES)


def alignment_order(dtype, channels):
    group = LANES // channels
    s = lax.broadcasted_iota(jnp.int32, (LANES, LANES), 0)
    t = lax.broadcasted_iota(jnp.int32, (LANES, LANES), 1)
    return (s == (t % channels) * group + t // channels).astype(dtype)


def pack_kernel(left_ref, right_ref, mask_ref, cot_ref, out_ref, held_ref):
    rows, width = left_ref.shape
    residues = cot_ref.shape[1]
    channels = width // LANES
    group = LANES // channels
    right_at, cot_at, mask_at, length = message_layout(rows, channels, residues)
    order = alignment_order(jnp.bfloat16, channels)
    mask = dot(mask_ref[...].astype(jnp.float32).astype(jnp.bfloat16), order, ((1,), (0,)))
    for source, first in ((left_ref, 0), (right_ref, right_at)):
        values = source[...].astype(jnp.float32)
        for i in range(rows):
            for k in range(channels):
                held_ref[k : k + 1, :] = values[i : i + 1, k * LANES : (k + 1) * LANES]
            turned = held_ref[...].T
            block = jnp.concatenate(
                [turned[g * channels : (g + 1) * channels] for g in range(group)], axis=1
            )
            block = block * mask[i : i + 1, :]
            out_ref[first + i * channels : first + (i + 1) * channels, :] = block.astype(
                jnp.bfloat16
            )
    for i in range(rows):
        out_ref[cot_at + i * residues : cot_at + (i + 1) * residues, :] = cot_ref[i]
    out_ref[mask_at:length, :] = jnp.concatenate(
        [mask, jnp.zeros((length - mask_at - rows, LANES), jnp.float32)], axis=0
    ).astype(jnp.bfloat16)


def main_kernel(rows, channels, residues, devices, me_ref, *refs):
    pieces = refs[:devices]
    weight_ref, bias_ref = refs[devices : devices + 2]
    pair_ref, left_ref, right_ref, gw_ref, gb_ref = refs[devices + 2 : devices + 7]
    (
        spread_ref, a_ref, b_ref, bn_ref, cott_f_ref, cott_ref, mask_f_ref,
        weight_f_ref, wl_ref, wr_ref, inv_ref, rhs_ref, prob_ref, cc_ref, lhs_ref,
    ) = refs[devices + 7 :]
    half = LANES // 2
    pairs = channels // 2
    right_at, cot_at, mask_at, _ = message_layout(rows, channels, residues)
    me = me_ref[0]
    bf = jnp.bfloat16

    mask_f_ref[...] = jnp.zeros_like(mask_f_ref)
    cott_f_ref[...] = jnp.zeros_like(cott_f_ref)
    total = jnp.zeros((rows * residues, LANES), jnp.float32)
    spread_ref[...] = jnp.zeros_like(spread_ref)
    for q, piece in enumerate(pieces):
        first = (me ^ q) * rows
        cot = piece[cot_at:mask_at, :].astype(jnp.float32)
        total = total + cot
        features = piece[0:cot_at, :].astype(jnp.float32)
        mask = piece[mask_at : mask_at + SUBLANES, :].astype(jnp.float32)
        for i in range(rows):
            at = first + i
            spread_ref[0, pl.ds(at, channels, stride=half), :] = features[
                i * channels : (i + 1) * channels
            ]
            spread_ref[1, pl.ds(at, channels, stride=half), :] = features[
                right_at + i * channels : right_at + (i + 1) * channels
            ]
            cott_f_ref[pl.ds(at, residues, stride=half), :] = cot[
                i * residues : (i + 1) * residues
            ]
            mask_f_ref[pl.ds(at, 1), :] = mask[i : i + 1]
        bn_ref[pl.ds(pl.multiple_of(first * channels, SUBLANES), rows * channels), :] = piece[
            right_at:cot_at, :
        ]
    a_ref[...] = spread_ref[0].astype(bf)
    b_ref[...] = spread_ref[1].astype(bf)
    cott_ref[...] = cott_f_ref[...].astype(bf)
    gb_ref[...] = jnp.sum(total, axis=0, keepdims=True) * (1.0 / residues)

    mask = mask_f_ref[...].astype(bf)
    counts = dot(mask, jnp.concatenate([mask, mask], axis=0), ((1,), (1,)))
    inv_ref[...] = 1.0 / jnp.maximum(counts, 1.0)

    weight_f_ref[...] = weight_ref[...].astype(jnp.float32)
    for h in range(pairs):
        for t in range(2):
            wl_ref[h * channels : (h + 1) * channels, t * LANES : (t + 1) * LANES] = weight_f_ref[
                pl.ds(2 * h + t, channels, stride=channels), :
            ].astype(bf)
            at = (2 * h + t) * channels
            wr_ref[h * channels : (h + 1) * channels, t * LANES : (t + 1) * LANES] = weight_ref[
                at : at + channels, :
            ]

    def norms():
        return [inv_ref[pl.ds(me * rows + i, 1), :] for i in range(rows)]

    def unfold(grad, out):
        group = LANES // channels
        own = mask_f_ref
        for i in range(rows):
            block = grad[i * channels : (i + 1) * channels] * own[pl.ds(me * rows + i, 1), :]
            stacked = jnp.concatenate(
                [block[:, g * channels : (g + 1) * channels] for g in range(group)], axis=0
            ).T
            for k in range(channels):
                out[i : i + 1, k * LANES : (k + 1) * LANES] = stacked[k : k + 1, :]

    def feature_gradient(w_ref, cots, other_ref, out):
        cc_ref[...] = jnp.zeros_like(cc_ref)
        for i, cot in enumerate(cots):
            for t in range(2):
                at = i * LANES + t * half
                cc_ref[at : at + cot.shape[0], t * LANES : (t + 1) * LANES] = cot
        grads = dot(w_ref[...], cc_ref[...], ((1,), (1,)))
        for i, inv in enumerate(norms()):
            scaled = (grads[:, i * LANES : (i + 1) * LANES] * inv).astype(bf)
            for h in range(pairs):
                lhs_ref[i * channels : (i + 1) * channels, h * LANES : (h + 1) * LANES] = scaled[
                    h * channels : (h + 1) * channels
                ]
        unfold(dot(lhs_ref[...], other_ref[...], ((1,), (0,))), out)

    own = pieces[0]
    feature_gradient(
        wl_ref,
        [own[cot_at + i * residues : cot_at + (i + 1) * residues, :] for i in range(rows)],
        b_ref,
        left_ref,
    )
    feature_gradient(
        wr_ref,
        [
            cott_ref[pl.ds(pl.multiple_of((me * rows + i) * half, half), half), :]
            for i in range(rows)
        ],
        a_ref,
        right_ref,
    )

    outer = dot(own[0:right_at, :], b_ref[...], ((1,), (1,)))
    probs = []
    for i, inv in enumerate(norms()):
        block = outer[i * channels : (i + 1) * channels]
        probs.append(
            jnp.concatenate(
                [
                    (block[:, h * LANES : (h + 1) * LANES] * inv).astype(bf)
                    for h in range(pairs)
                ],
                axis=0,
            )
        )
    for i in range(rows):
        both = dot(probs[i], wl_ref[...], ((0,), (0,)))
        pair_ref[i] = (
            both[0:residues, 0:LANES] + both[half : half + residues, LANES:] + bias_ref[...]
        ).astype(bf)

    rhs_ref[...] = jnp.zeros_like(rhs_ref)
    for j in range(residues):
        for t in range(2):
            at = j * LANES + t * half
            rhs_ref[at : at + half, t * LANES : (t + 1) * LANES] = cott_ref[
                j * half : (j + 1) * half, :
            ]
    step = math.gcd(residues, SUBLANES)
    acc = None
    for first in range(0, residues, step):
        outer = dot(
            bn_ref[first * channels : (first + step) * channels, :], a_ref[...], ((1,), (1,))
        )
        for j in range(step):
            inv = inv_ref[first + j : first + j + 1, :]
            block = outer[j * channels : (j + 1) * channels]
            for h in range(pairs):
                prob_ref[h * channels : (h + 1) * channels, j * LANES : (j + 1) * LANES] = (
                    block[:, h * LANES : (h + 1) * LANES] * inv
                ).astype(bf)
        part = dot(
            prob_ref[...], rhs_ref[first * LANES : (first + step) * LANES, :], ((1,), (0,))
        )
        acc = part if acc is None else acc + part
    acc = acc * (1.0 / residues)
    for h in range(pairs):
        for t in range(2):
            at = (2 * h + t) * channels
            gw_ref[at : at + channels, :] = acc[
                h * channels : (h + 1) * channels, t * LANES : (t + 1) * LANES
            ]


def gathered(message, devices):
    messages = {0: message}
    step = devices // 2
    while step:
        partners = [(i, i ^ step) for i in range(devices)]
        for q in list(messages):
            messages[q ^ step] = lax.ppermute(messages[q], "row", partners)
        step //= 2
    return [messages[q] for q in range(devices)]


def exchanged(left, right, mask, weight, bias, cotangent):
    rows, width = left.shape
    channels = width // mask.shape[1]
    residues = cotangent.shape[1]
    devices = lax.axis_size("row")
    half = LANES // 2
    pairs = channels // 2
    length = message_layout(rows, channels, residues)[-1]
    step = math.gcd(residues, SUBLANES)
    bf, f32 = jnp.bfloat16, jnp.float32
    vmem = pl.BlockSpec(memory_space=pltpu.VMEM)
    message = pl.pallas_call(
        pack_kernel,
        out_shape=jax.ShapeDtypeStruct((length, LANES), bf),
        in_specs=[vmem] * 4,
        out_specs=vmem,
        scratch_shapes=[pltpu.VMEM((channels, LANES), f32)],
        name="pack",
    )(left, right, mask, cotangent)
    messages = gathered(message, devices)
    me = lax.axis_index("row").astype(jnp.int32).reshape(1)
    pair, left_grad, right_grad, weight_grad, bias_grad = pl.pallas_call(
        lambda *refs: main_kernel(rows, channels, residues, devices, *refs),
        out_shape=(
            jax.ShapeDtypeStruct(cotangent.shape, bf),
            jax.ShapeDtypeStruct(left.shape, f32),
            jax.ShapeDtypeStruct(right.shape, f32),
            jax.ShapeDtypeStruct(weight.shape, f32),
            jax.ShapeDtypeStruct((1, LANES), f32),
        ),
        in_specs=[pl.BlockSpec(memory_space=pltpu.SMEM)] + [vmem] * (devices + 2),
        out_specs=(vmem,) * 5,
        scratch_shapes=[
            pltpu.VMEM((2, channels * half, LANES), f32),
            pltpu.VMEM((channels * half, LANES), bf),
            pltpu.VMEM((channels * half, LANES), bf),
            pltpu.VMEM((residues * channels, LANES), bf),
            pltpu.VMEM((residues * half, LANES), f32),
            pltpu.VMEM((residues * half, LANES), bf),
            pltpu.VMEM((half, LANES), f32),
            pltpu.VMEM(weight.shape, f32),
            pltpu.VMEM((pairs * channels, 2 * LANES), bf),
            pltpu.VMEM((pairs * channels, 2 * LANES), bf),
            pltpu.VMEM((half, LANES), f32),
            pltpu.VMEM((residues * LANES, 2 * LANES), bf),
            pltpu.VMEM((pairs * channels, step * LANES), bf),
            pltpu.VMEM((rows * LANES, 2 * LANES), bf),
            pltpu.VMEM((rows * channels, pairs * LANES), bf),
        ],
        name="products",
    )(me, *messages, weight, bias.reshape(1, LANES))
    return pair, left_grad, right_grad, weight_grad, bias_grad.reshape(LANES)


def solution(mesh):
    devices = mesh.shape["row"]

    def run(*arrays):
        return (exchanged if fits(devices, *arrays) else reduced)(*arrays)

    in_specs = (
        P(("groups", "row"), None),
        P(("groups", "row"), None),
        P(("groups", "row"), None),
        P(),
        P(),
        P(("groups", "row"), None, None),
    )
    out_specs = (
        P(("groups", "row"), None, None),
        P(("groups", "row"), None),
        P(("groups", "row"), None),
        P("groups", None),
        P("groups"),
    )
    return jax.shard_map(run, mesh=mesh, in_specs=in_specs, out_specs=out_specs, check_vma=False)
```
